256 devices in a mesh: rows: 32 (over y, x, z_lo), tm: 8 (over z_hi, core).
Axes of the slice: x: 4, y: 4, z: 8 (z_hi: 4, z_lo: 2; z = z_hi * 2 + z_lo), core: 2. Of those that a mesh axis runs over, the one named last changes fastest.
Arguments:
- video: bfloat16 [32, 128, 96, 192], P('tm', 'rows'), may hold values from -6 to 6
- gains: float32 [4, 192], replicated, may hold values from 0.1 to 1.9
- kernels: bfloat16 [4, 3, 3, 3, 192, 192], replicated, may hold values from -0.078125 to 0.078125
Outputs:
- encoded: bfloat16 [32, 128, 96, 192], P('tm', 'rows')
The draws below stay inside these ranges and needn't reach their ends.
All inputs are finite; a program needn't handle non-finite values.
Results may differ from the reference program's by a relative error of at most 0.0065.
Values may be sent and summed in bfloat16 or wider, within the bound.
A program may use at most 128 MiB of HBM per device.

```python
import jax
import jax.numpy as jnp
from jax import lax

C = 192
W = 96
FRAMES = 32
HEIGHT = 128


def block_scale(own_key, dims, pieces, low, top_value):
    factor_of = 1.0
    for position, parts in pieces:
        steps = jax.random.uniform(jax.random.fold_in(jax.random.fold_in(own_key, 6), position), (parts,), jnp.float32, low / len(pieces), top_value / len(pieces))
        factor_of = factor_of * jnp.repeat(jnp.exp(steps), dims[position] // parts).reshape((-1,) + (1,) * (len(dims) - 1 - position))
    return factor_of


def normal_values(rng, shape, scale, reach, pieces=(), dtype=jnp.bfloat16):
    drawn = jax.random.normal(rng, shape, jnp.float32) * scale
    if len(pieces) > 0:
        drawn = block_scale(rng, shape, pieces, -0.22, 0.18) * drawn
    return jnp.clip(drawn, min=-reach, max=reach).astype(dtype)


def setup_inputs(seed: int = 0) -> dict:
    splits = jax.random.split(jax.random.key(seed), 4)
    video = normal_values(splits[0], (FRAMES, HEIGHT, W, C), 1.0, 6.0, ((0, 8), (1, 32)))
    gains = jnp.clip(1.0 + 0.18 * jax.random.normal(splits[1], (4, C), jnp.float32), 0.1, 1.9)
    kernels = normal_values(splits[2], (4, 3, 3, 3, C, C), (27 * C) ** -0.5, 0.078125)
    return {"video": video, "gains": gains, "kernels": kernels}


def activate(field, gain):
    values = field.astype(jnp.float32)
    scaled = values * lax.rsqrt(lax.optimization_barrier(jnp.mean(values * values, axis=-1, keepdims=True)) + 1e-06) * gain.astype(jnp.float32)
    return jax.nn.silu(scaled).astype(jnp.bfloat16)

def convolve(field, kernel):
    result = lax.conv_general_dilated(field.astype(jnp.float32)[None], kernel.astype(jnp.float32), (1, 1, 1), [(2, 0), (1, 1), (1, 1)], dimension_numbers=('NDHWC', 'DHWIO', 'NDHWC'), precision=lax.Precision.HIGHEST)
    return result[0]

def reference(video, gains, kernels):
    hidden = video
    for block in range(2):
        first = activate(hidden, gains[2 * block])
        second = activate(convolve(first, kernels[2 * block]), gains[2 * block + 1])
        branch = convolve(second, kernels[2 * block + 1])
        hidden = (hidden.astype(jnp.float32) + branch).astype(jnp.bfloat16)
    return hidden
```

```python
import jax
import jax.numpy as jnp
from jax import lax
from jax.experimental import pallas as pl
from jax.experimental.pallas import tpu as pltpu
from jax.sharding import PartitionSpec as P

MESH = pl.DeviceIdType.MESH
BF = jnp.bfloat16
F32 = jnp.float32
F, R, W, C = 4, 4, 96, 192
LO, HI = 128, 64
K1 = 640


def norm_act(value, gain):
    lo, hi = value
    mean = jnp.sum(lo * lo + hi * hi, axis=-1, keepdims=True) * (1.0 / C)
    scale = lax.rsqrt(mean + 1e-06)
    return tuple(s / (1.0 + jnp.exp(-s)) for s in (lo * scale * gain[0], hi * scale * gain[1]))


def lane_id():
    return lax.broadcasted_iota(jnp.int32, (W, LO), 1)


def join(first, second):
    both = first[1] + pltpu.roll(second[1], HI, 1)
    return jnp.concatenate([first[0].astype(BF), second[0].astype(BF), both.astype(BF)], axis=1)


def split(packet):
    values = packet.astype(F32)
    tail = values[:, 2 * LO :]
    low = lane_id() < HI
    first = jnp.where(low, tail, 0.0)
    second = jnp.where(low, pltpu.roll(tail, HI, 1), 0.0)
    return (values[:, :LO], first), (values[:, LO : 2 * LO], second)


def widen(ref, value):
    column = lax.broadcasted_iota(jnp.int32, (W, LO), 0)
    lo, hi = value

    def left(v):
        return jnp.where(column == 0, 0.0, pltpu.roll(v, 1, 0))

    def right(v):
        return jnp.where(column == W - 1, 0.0, pltpu.roll(v, W - 1, 0))

    ref[:, 0:128] = left(lo).astype(BF)
    ref[:, 128:256] = lo.astype(BF)
    ref[:, 256:384] = right(lo).astype(BF)
    ref[:, 384:512] = (left(hi) + pltpu.roll(hi, HI, 1)).astype(BF)
    ref[:, 512:640] = right(hi).astype(BF)


def place():
    r, t = lax.axis_index("rows"), lax.axis_index("tm")
    r2, t2 = lax.div(r, 2), lax.div(t, 2)
    r1, t1 = lax.rem(r, 2), lax.rem(t, 2)
    return 2 * t2 + r1, 2 * r2 + t1, (2 * r2 + t1, 2 * t2 + r1), r1 != t1


def device(slab, strip):
    s2, q2 = lax.div(slab, 2), lax.div(strip, 2)
    return 2 * q2 + lax.rem(slab, 2), 2 * s2 + lax.rem(strip, 2)


def kernel(
    video, gains, kernels, out,
    vid, res, X, Wt, acc, own, swap_out, swap_in, A, T, N, Q,
    w_sem, v_sem, l_sem, o_sem, sw_send, sw_recv, t_send, t_recv, n_send, n_recv, q_send, q_recv,
):
    slab, strip, partner, swaps = place()
    has_prev, has_next = slab > 0, slab < 7
    has_up, has_down = strip > 0, strip < 31
    prev, follow = device(slab - 1, strip), device(slab + 1, strip)
    up, down = device(slab, strip - 1), device(slab, strip + 1)

    loads = [pltpu.make_async_copy(video.at[pl.ds(2, 2)], vid.at[pl.ds(2, 2)], v_sem.at[1]),
             pltpu.make_async_copy(video.at[pl.ds(0, 2)], vid.at[pl.ds(0, 2)], v_sem.at[0])]
    for copy in loads:
        copy.start()
    weights = []
    for k in range(4):
        group = [pltpu.make_async_copy(
            kernels.at[k, :, :, :, pl.ds(0, LO), :], Wt.at[k, :, :, pl.ds(0, 3), :, :], w_sem.at[k, 0])]
        for q in range(3):
            group.append(pltpu.make_async_copy(
                kernels.at[k, :, :, q, pl.ds(LO, HI), :],
                Wt.at[k, :, :, 3 + q // 2, pl.ds(HI * (q % 2), HI), :],
                w_sem.at[k, 1 + q]))
        weights.append(group)
    for copy in weights[0]:
        copy.start()

    barrier = pltpu.get_barrier_semaphore()
    count = jnp.int32(0)
    for there, target in ((has_prev, prev), (has_next, follow), (has_up, up), (has_down, down), (swaps, partner)):
        count = count + there.astype(jnp.int32)

        @pl.when(there)
        def _(target=target):
            pl.semaphore_signal(barrier, inc=1, device_id=target, device_id_type=MESH)

    pl.semaphore_wait(barrier, count)

    def remote(src, dst, send, recv, target):
        return pltpu.make_async_remote_copy(
            src_ref=src, dst_ref=dst, send_sem=send, recv_sem=recv, device_id=target, device_id_type=MESH)

    def exchange(source, sink, n, p):
        copy = remote(source.at[p], sink.at[p], sw_send.at[n, p], sw_recv.at[n, p], partner)
        local = pltpu.make_async_copy(source.at[p], sink.at[p], l_sem.at[n, p])
        return copy, local

    def begin(pair):
        copy, local = pair

        @pl.when(swaps)
        def _():
            copy.start()

        @pl.when(jnp.logical_not(swaps))
        def _():
            local.start()

    def finish(pair):
        copy, local = pair

        @pl.when(swaps)
        def _():
            copy.wait_recv()

        @pl.when(jnp.logical_not(swaps))
        def _():
            local.wait()

    inward = {}
    for p, load in ((1, loads[0]), (0, loads[1])):
        load.wait()

        @pl.loop(0, R)
        def _(r, p=p):
            pair = []
            for f in range(2):
                whole = vid[2 * p + f, r].astype(F32)
                whole = jnp.concatenate([whole, jnp.zeros((W, HI), F32)], axis=1)
                pair.append((whole[:, :LO], whole[:, LO:]))
            own[p, r] = join(*pair)

        inward[p] = exchange(own, swap_in, 0, p)
        begin(inward[p])

    for k in range(1, 4):
        for copy in weights[k]:
            copy.start()
    for s in range(2):
        X[s, 0:2] = jnp.zeros((2, R + 2, W, K1), BF)

        @pl.loop(2, F + 2)
        def _(f, s=s):
            X[s, f, 0] = jnp.zeros((W, K1), BF)
            X[s, f, R + 1] = jnp.zeros((W, K1), BF)

    Wt[:, :, :, 4, HI:, :] = jnp.zeros((4, 3, 3, LO - HI, C), BF)

    def gain(k):
        row = jnp.concatenate([gains[k : k + 1, :], jnp.zeros((1, HI), F32)], axis=1)
        return row[:, :LO], row[:, LO:]

    def frames_copy(j, r):
        return remote(A.at[j, 1, r], T.at[j, r], t_send.at[j, r], t_recv.at[j, r], follow)

    def row_copy(j, p, side):
        return remote(A.at[j, p, 3 * side], N.at[j, p, 1 - side], n_send.at[j, p, side], n_recv.at[j, p, 1 - side],
                      (up, down)[side])

    def corner_copy(j, side):
        return remote(T.at[j, 3 * side], Q.at[j, 1 - side], q_send.at[j, side], q_recv.at[j, 1 - side],
                      (up, down)[side])

    def send(j, p):
        for side, there in ((0, has_up), (1, has_down)):
            @pl.when(there)
            def _(side=side):
                row_copy(j, p, side).start()
        if p == 1:
            @pl.when(has_next)
            def _():
                for r in (0, 3, 1, 2):
                    frames_copy(j, r).start()

    def emit(j, p, r, pair):
        for f in range(2):
            widen(X.at[j % 2, 2 + 2 * p + f, r + 1], pair[f])
        A[j, p, r] = join(*pair)

    def widen_packet(ref, j, f, r):
        pair = split(ref[...])
        for i in range(2):
            widen(X.at[j % 2, f + i, r], pair[i])

    def take_rows(j):
        for side, there in ((0, has_up), (1, has_down)):
            @pl.when(there)
            def _(side=side):
                for p in (1, 0):
                    row_copy(j, p, 1 - side).wait_recv()
                    widen_packet(N.at[j, p, side], j, 2 + 2 * p, 5 * side)

    def take_frames(j):
        @pl.when(has_prev)
        def _():
            for side, there in ((0, has_up), (1, has_down)):
                frames_copy(j, 3 * side).wait_recv()

                @pl.when(there)
                def _(side=side):
                    corner_copy(j, side).start()
            for r in (1, 2):
                frames_copy(j, r).wait_recv()

            @pl.loop(0, R)
            def _(r):
                widen_packet(T.at[j, r], j, 0, r + 1)

            for side, there in ((0, has_up), (1, has_down)):
                @pl.when(there)
                def _(side=side):
                    corner_copy(j, 1 - side).wait_recv()
                    widen_packet(Q.at[j, side], j, 0, 5 * side)

    def convolve(j, p):
        s = j % 2
        parts = [X[s, 2 * p + dt : 2 * p + dt + 2, dr : dr + R].reshape(2 * R * W, K1)
                 for dt in range(3) for dr in range(3)]
        acc[...] = jnp.dot(
            jnp.concatenate(parts, axis=1), Wt[j].reshape(9 * K1, C), preferred_element_type=F32
        ).reshape(2, R, W, C)

    def sums(f, r):
        return acc[f, r, :, 0:LO], jnp.concatenate([acc[f, r, :, LO:C], jnp.zeros((W, HI), F32)], axis=1)

    def after(j, p):
        g = gain(j + 1) if j < 3 else None

        @pl.loop(0, R)
        def _(r):
            pair = [sums(f, r) for f in range(2)]
            if j % 2 == 1:
                old = split(swap_in[p, r])
                pair = [tuple((a + b).astype(BF).astype(F32) for a, b in zip(*both)) for both in zip(old, pair)]
                swap_in[p, r] = join(*pair)
            if j < 3:
                emit(j + 1, p, r, [norm_act(v, g) for v in pair])

    g0 = gain(0)
    for p in (1, 0):
        finish(inward[p])

        @pl.loop(0, R)
        def _(r, p=p):
            emit(0, p, r, [norm_act(v, g0) for v in split(swap_in[p, r])])

        send(0, p)

    outward = {}
    for j in range(4):
        take_rows(j)
        for copy in weights[j]:
            copy.wait()
        for p in (1, 0):
            if p == 0:
                take_frames(j)
            convolve(j, p)
            after(j, p)
            if j < 3:
                send(j + 1, p)
            else:
                outward[p] = exchange(swap_in, swap_out, 1, p)
                begin(outward[p])

    stores = []
    for p in (1, 0):
        finish(outward[p])

        @pl.loop(0, R)
        def _(r, p=p):
            pair = split(swap_out[p, r])
            for f in range(2):
                res[2 * p + f, r, :, 0:LO] = pair[f][0].astype(BF)
                res[2 * p + f, r, :, LO:C] = pair[f][1][:, :HI].astype(BF)

        store = pltpu.make_async_copy(res.at[pl.ds(2 * p, 2)], out.at[pl.ds(2 * p, 2)], o_sem.at[p])
        store.start()
        stores.append(store)

    @pl.when(swaps)
    def _():
        for p in (1, 0):
            inward[p][0].wait_send()
            outward[p][0].wait_send()

    for j in range(4):
        for side, there in ((0, has_up), (1, has_down)):
            @pl.when(there)
            def _(j=j, side=side):
                for p in (1, 0):
                    row_copy(j, p, side).wait_send()

                @pl.when(has_prev)
                def _():
                    corner_copy(j, side).wait_send()

        @pl.when(has_next)
        def _(j=j):
            for r in range(R):
                frames_copy(j, r).wait_send()

    for store in stores:
        store.wait()


def body(video, gains, kernels):
    packet = (W, 2 * C)
    dma = pltpu.SemaphoreType.DMA
    return pl.pallas_call(
        kernel,
        out_shape=jax.ShapeDtypeStruct(video.shape, video.dtype),
        in_specs=[
            pl.BlockSpec(memory_space=pl.ANY),
            pl.BlockSpec(memory_space=pltpu.VMEM),
            pl.BlockSpec(memory_space=pl.ANY),
        ],
        out_specs=pl.BlockSpec(memory_space=pl.ANY),
        scratch_shapes=[
            pltpu.VMEM((F, R, W, C), BF),
            pltpu.VMEM((F, R, W, C), BF),
            pltpu.VMEM((2, F + 2, R + 2, W, K1), BF),
            pltpu.VMEM((4, 3, 3, 5, LO, C), BF),
            pltpu.VMEM((2, R, W, C), F32),
            pltpu.VMEM((2, R) + packet, BF),
            pltpu.VMEM((2, R) + packet, BF),
            pltpu.VMEM((2, R) + packet, BF),
            pltpu.VMEM((4, 2, R) + packet, BF),
            pltpu.VMEM((4, R) + packet, BF),
            pltpu.VMEM((4, 2, 2) + packet, BF),
            pltpu.VMEM((4, 2) + packet, BF),
            dma((4, 4)), dma((2,)), dma((2, 2)), dma((2,)),
            dma((2, 2)), dma((2, 2)),
            dma((4, R)), dma((4, R)),
            dma((4, 2, 2)), dma((4, 2, 2)),
            dma((4, 2)), dma((4, 2)),
        ],
        compiler_params=pltpu.CompilerParams(
            collective_id=0, has_side_effects=True, vmem_limit_bytes=56 << 20),
        name="blocks",
    )(video, gains, kernels)


def solution(mesh):
    in_specs = (P("tm", "rows", None, None), P(), P())
    out_specs = P("tm", "rows", None, None)
    return jax.shard_map(body, mesh=mesh, in_specs=in_specs, out_specs=out_specs, check_vma=False)
```

```python
import jax
import jax.numpy as jnp
from jax import lax
from jax.experimental import pallas as pl
from jax.experimental.pallas import tpu as pltpu
from jax.sharding import PartitionSpec as P

MESH = pl.DeviceIdType.MESH
BF = jnp.bfloat16
F32 = jnp.float32
F, R, W, C = 4, 4, 96, 192
LO, HI = 128, 64
K1 = 640


def norm_act(value, gain):
    lo, hi = value
    mean = jnp.sum(lo * lo + hi * hi, axis=-1, keepdims=True) * (1.0 / C)
    scale = lax.rsqrt(mean + 1e-06)
    return tuple(s / (1.0 + jnp.exp(-s)) for s in (lo * scale * gain[0], hi * scale * gain[1]))


def lane_id():
    return lax.broadcasted_iota(jnp.int32, (W, LO), 1)


def join(first, second):
    both = first[1] + pltpu.roll(second[1], HI, 1)
    return jnp.concatenate([first[0].astype(BF), second[0].astype(BF), both.astype(BF)], axis=1)


def split(packet):
    values = packet.astype(F32)
    tail = values[:, 2 * LO :]
    low = lane_id() < HI
    first = jnp.where(low, tail, 0.0)
    second = jnp.where(low, pltpu.roll(tail, HI, 1), 0.0)
    return (values[:, :LO], first), (values[:, LO : 2 * LO], second)


def widen(ref, value):
    column = lax.broadcasted_iota(jnp.int32, (W, LO), 0)
    lo, hi = value

    def left(v):
        return jnp.where(column == 0, 0.0, pltpu.roll(v, 1, 0))

    def right(v):
        return jnp.where(column == W - 1, 0.0, pltpu.roll(v, W - 1, 0))

    ref[:, 0:128] = left(lo).astype(BF)
    ref[:, 128:256] = lo.astype(BF)
    ref[:, 256:384] = right(lo).astype(BF)
    ref[:, 384:512] = (left(hi) + pltpu.roll(hi, HI, 1)).astype(BF)
    ref[:, 512:640] = right(hi).astype(BF)


def place():
    r, t = lax.axis_index("rows"), lax.axis_index("tm")
    r2, t2 = lax.div(r, 2), lax.div(t, 2)
    r1, t1 = lax.rem(r, 2), lax.rem(t, 2)
    return 2 * t2 + r1, 2 * r2 + t1, (2 * r2 + t1, 2 * t2 + r1), r1 != t1


def device(slab, strip):
    s2, q2 = lax.div(slab, 2), lax.div(strip, 2)
    return 2 * q2 + lax.rem(slab, 2), 2 * s2 + lax.rem(strip, 2)


def kernel(
    video, gains, kernels, out,
    vid, res, X, Wt, acc, own, swap_out, swap_in, A, T, N, Q,
    w_sem, v_sem, l_sem, o_sem, sw_send, sw_recv, t_send, t_recv, n_send, n_recv, q_send, q_recv,
):
    slab, strip, partner, swaps = place()
    has_prev, has_next = slab > 0, slab < 7
    has_up, has_down = strip > 0, strip < 31
    prev, follow = device(slab - 1, strip), device(slab + 1, strip)
    up, down = device(slab, strip - 1), device(slab, strip + 1)

    loads = [pltpu.make_async_copy(video.at[pl.ds(2, 2)], vid.at[pl.ds(2, 2)], v_sem.at[1]),
             pltpu.make_async_copy(video.at[pl.ds(0, 2)], vid.at[pl.ds(0, 2)], v_sem.at[0])]
    for copy in loads:
        copy.start()

    def weights(k):
        copies = [pltpu.make_async_copy(
            kernels.at[k, :, :, :, pl.ds(0, LO), :], Wt.at[k, :, :, pl.ds(0, 3), :, :], w_sem.at[k, 0])]
        for q in range(3):
            copies.append(pltpu.make_async_copy(
                kernels.at[k, :, :, q, pl.ds(LO, HI), :],
                Wt.at[k, :, :, 3 + q // 2, pl.ds(HI * (q % 2), HI), :],
                w_sem.at[k, 1 + q]))
        return copies

    zero = jnp.zeros((W, 2 * C), BF)
    for side, there in ((0, has_up), (1, has_down)):
        @pl.when(jnp.logical_not(there))
        def _(side=side):
            @pl.loop(0, 4)
            def _(j):
                N[j, 0, side] = zero
                N[j, 1, side] = zero
                Q[j, side] = zero

    @pl.when(jnp.logical_not(has_prev))
    def _():
        @pl.loop(0, 4)
        def _(j):
            for r in range(R):
                T[j, r] = zero
            for side in range(2):
                Q[j, side] = zero

    barrier = pltpu.get_barrier_semaphore()
    count = jnp.int32(0)
    for there, target in ((has_prev, prev), (has_next, follow), (has_up, up), (has_down, down), (swaps, partner)):
        count = count + there.astype(jnp.int32)

        @pl.when(there)
        def _(target=target):
            pl.semaphore_signal(barrier, inc=1, device_id=target, device_id_type=MESH)

    pl.semaphore_wait(barrier, count)

    def remote(src, dst, send, recv, target):
        return pltpu.make_async_remote_copy(
            src_ref=src, dst_ref=dst, send_sem=send, recv_sem=recv, device_id=target, device_id_type=MESH)

    def exchange(source, sink, n, p, r=None):
        at = (p,) if r is None else (p, r)
        sem = (n, p, 0) if r is None else (n, p, r)
        copy = remote(source.at[at], sink.at[at], sw_send.at[sem], sw_recv.at[sem], partner)
        local = pltpu.make_async_copy(source.at[at], sink.at[at], l_sem.at[sem])
        return copy, local

    def begin(pair):
        copy, local = pair

        @pl.when(swaps)
        def _():
            copy.start()

        @pl.when(jnp.logical_not(swaps))
        def _():
            local.start()

    def finish(pair):
        copy, local = pair

        @pl.when(swaps)
        def _():
            copy.wait_recv()

        @pl.when(jnp.logical_not(swaps))
        def _():
            local.wait()

    def packed(r, p):
        pair = []
        for f in range(2):
            whole = vid[2 * p + f, r].astype(F32)
            whole = jnp.concatenate([whole, jnp.zeros((W, HI), F32)], axis=1)
            pair.append((whole[:, :LO], whole[:, LO:]))
        own[p, r] = join(*pair)

    for q, load in enumerate(loads):
        p = 1 - q
        load.wait()

        @pl.loop(0, R)
        def _(r, p=p):
            packed(r, p)

        begin(exchange(own, swap_in, 0, p))

    for copy in weights(0):
        copy.start()

    @pl.loop(1, 4)
    def _(k):
        for copy in weights(k):
            copy.start()

    @pl.loop(0, 36)
    def _(i):
        Wt[lax.div(i, 9), lax.div(lax.rem(i, 9), 3), lax.rem(i, 3), 4, HI:, :] = jnp.zeros((LO - HI, C), BF)

    def gain(k):
        row = jnp.concatenate([gains[pl.ds(k, 1), :], jnp.zeros((1, HI), F32)], axis=1)
        return row[:, :LO], row[:, LO:]

    def frames_copy(j, r):
        return remote(A.at[j, 1, r], T.at[j, r], t_send.at[j, r], t_recv.at[j, r], follow)

    def row_copy(j, p, side):
        return remote(A.at[j, p, 3 * side], N.at[j, p, 1 - side], n_send.at[j, p, side], n_recv.at[j, p, 1 - side],
                      (up, down)[side])

    def corner_copy(j, side):
        return remote(T.at[j, 3 * side], Q.at[j, 1 - side], q_send.at[j, side], q_recv.at[j, 1 - side],
                      (up, down)[side])

    sides = ((0, has_up), (1, has_down))

    def send_rows(j, p):
        for side, there in sides:
            @pl.when(there)
            def _(side=side):
                row_copy(j, p, side).start()

    def send_frames(j):
        @pl.when(has_next)
        def _():
            for r in (0, 3, 1, 2):
                frames_copy(j, r).start()

    def emit(j, p, r, pair):
        for f in range(2):
            widen(X.at[lax.rem(j, 2), 2 + 2 * p + f, r + 1], pair[f])
        A[j, p, r] = join(*pair)

    def widen_packet(ref, j, f, r):
        pair = split(ref[...])
        for i in range(2):
            widen(X.at[lax.rem(j, 2), f + i, r], pair[i])

    def take_rows(j):
        for side, there in sides:
            @pl.when(there)
            def _(side=side):
                for p in (1, 0):
                    row_copy(j, p, 1 - side).wait_recv()

        @pl.loop(0, 4)
        def _(i):
            p, side = lax.div(i, 2), lax.rem(i, 2)
            widen_packet(N.at[j, p, side], j, 2 + 2 * p, 5 * side)

    def forward_corners(j):
        @pl.when(has_prev)
        def _():
            for side, there in sides:
                frames_copy(j, 3 * side).wait_recv()

                @pl.when(there)
                def _(side=side):
                    corner_copy(j, side).start()

    def take_frames(j):
        @pl.when(has_prev)
        def _():
            for r in (1, 2):
                frames_copy(j, r).wait_recv()

        @pl.loop(0, R)
        def _(r):
            widen_packet(T.at[j, r], j, 0, r + 1)

        for side, there in sides:
            @pl.when(jnp.logical_and(there, has_prev))
            def _(side=side):
                corner_copy(j, 1 - side).wait_recv()

        @pl.loop(0, 2)
        def _(side):
            widen_packet(Q.at[j, side], j, 0, 5 * side)

    def convolve(j, p, rows):
        s = lax.rem(j, 2)
        parts = []
        for dt in range(3):
            for dr in range(3):
                parts.append(jnp.concatenate(
                    [X[s, 2 * p + dt + f, r + dr] for f in range(2) for r in rows], axis=0))
        acc[...] = jnp.dot(
            jnp.concatenate(parts, axis=1), Wt[j].reshape(9 * K1, C), preferred_element_type=F32
        ).reshape(2, 2, W, C)

    def sums(f, i):
        return acc[f, i, :, 0:LO], jnp.concatenate([acc[f, i, :, LO:C], jnp.zeros((W, HI), F32)], axis=1)

    def after(j, p, rows):
        @pl.when(lax.rem(j, 2) == 1)
        def _():
            @pl.loop(0, 2)
            def _(i):
                r = rows[0] + i * (rows[1] - rows[0])
                old = split(swap_in[p, r])
                pair = [tuple((a + b).astype(BF).astype(F32) for a, b in zip(old[f], sums(f, i))) for f in range(2)]
                swap_in[p, r] = join(*pair)
                for f in range(2):
                    acc[f, i, :, 0:LO] = pair[f][0]
                    acc[f, i, :, LO:C] = pair[f][1][:, :HI]

        @pl.when(j < 3)
        def _():
            g = gain(j + 1)

            @pl.loop(0, 2)
            def _(i):
                r = rows[0] + i * (rows[1] - rows[0])
                emit(j + 1, p, r, [norm_act(sums(f, i), g) for f in range(2)])

    def outward(p, r):
        return exchange(swap_in, swap_out, 1, p, r)

    g0 = gain(0)

    @pl.loop(0, 2)
    def _(q):
        p = 1 - q
        finish(exchange(own, swap_in, 0, p))

        @pl.loop(0, R)
        def _(r):
            emit(0, p, r, [norm_act(v, g0) for v in split(swap_in[p, r])])

        send_rows(0, p)

        @pl.when(p == 1)
        def _():
            send_frames(0)

    def unit(u):
        first = jnp.where(jnp.logical_or(u == 1, u == 2), 0, 1)
        return 1 - lax.div(u, 2), (first, 3 - first)

    @pl.loop(0, 4)
    def _(j):
        for copy in weights(j):
            copy.wait()

        @pl.loop(0, 4)
        def _(u):
            p, rows = unit(u)

            @pl.when(u == 1)
            def _():
                take_rows(j)
                forward_corners(j)

            @pl.when(u == 2)
            def _():
                take_frames(j)

            convolve(j, p, rows)
            after(j, p, rows)

            @pl.when(jnp.logical_and(j < 3, jnp.logical_or(u == 1, u == 2)))
            def _():
                send_rows(j + 1, p)

            @pl.when(jnp.logical_and(j < 3, u == 1))
            def _():
                send_frames(j + 1)

            @pl.when(j == 3)
            def _():
                for r in rows:
                    begin(outward(p, r))

    def stored(p, r):
        return pltpu.make_async_copy(res.at[pl.ds(2 * p, 2), r], out.at[pl.ds(2 * p, 2), r], o_sem.at[p, r])

    @pl.loop(0, 8)
    def _(i):
        p, rows = unit(lax.div(i, 2))
        r = rows[0] + lax.rem(i, 2) * (rows[1] - rows[0])
        finish(outward(p, r))
        pair = split(swap_out[p, r])
        for f in range(2):
            res[2 * p + f, r, :, 0:LO] = pair[f][0].astype(BF)
            res[2 * p + f, r, :, LO:C] = pair[f][1][:, :HI].astype(BF)
        stored(p, r).start()

    @pl.when(swaps)
    def _():
        @pl.loop(0, 2)
        def _(p):
            exchange(own, swap_in, 0, p)[0].wait_send()

            @pl.loop(0, R)
            def _(r):
                outward(p, r)[0].wait_send()

    @pl.loop(0, 4)
    def _(j):
        for side, there in sides:
            @pl.when(there)
            def _(side=side):
                for p in (1, 0):
                    row_copy(j, p, side).wait_send()

            @pl.when(jnp.logical_and(there, has_prev))
            def _(side=side):
                corner_copy(j, side).wait_send()

        @pl.when(has_next)
        def _():
            for r in range(R):
                frames_copy(j, r).wait_send()

    @pl.loop(0, 2)
    def _(p):
        @pl.loop(0, R)
        def _(r):
            stored(p, r).wait()


def body(video, gains, kernels):
    packet = (W, 2 * C)
    dma = pltpu.SemaphoreType.DMA
    return pl.pallas_call(
        kernel,
        out_shape=jax.ShapeDtypeStruct(video.shape, video.dtype),
        in_specs=[
            pl.BlockSpec(memory_space=pl.ANY),
            pl.BlockSpec(memory_space=pltpu.VMEM),
            pl.BlockSpec(memory_space=pl.ANY),
        ],
        out_specs=pl.BlockSpec(memory_space=pl.ANY),
        scratch_shapes=[
            pltpu.VMEM((F, R, W, C), BF),
            pltpu.VMEM((F, R, W, C), BF),
            pltpu.VMEM((2, F + 2, R + 2, W, K1), BF),
            pltpu.VMEM((4, 3, 3, 5, LO, C), BF),
            pltpu.VMEM((2, 2, W, C), F32),
            pltpu.VMEM((2, R) + packet, BF),
            pltpu.VMEM((2, R) + packet, BF),
            pltpu.VMEM((2, R) + packet, BF),
            pltpu.VMEM((4, 2, R) + packet, BF),
            pltpu.VMEM((4, R) + packet, BF),
            pltpu.VMEM((4, 2, 2) + packet, BF),
            pltpu.VMEM((4, 2) + packet, BF),
            dma((4, 4)), dma((2,)), dma((2, 2, R)), dma((2, R)),
            dma((2, 2, R)), dma((2, 2, R)),
            dma((4, R)), dma((4, R)),
            dma((4, 2, 2)), dma((4, 2, 2)),
            dma((4, 2)), dma((4, 2)),
        ],
        compiler_params=pltpu.CompilerParams(
            collective_id=0, has_side_effects=True, vmem_limit_bytes=56 << 20),
        name="blocks",
    )(video, gains, kernels)


def solution(mesh):
    in_specs = (P("tm", "rows", None, None), P(), P())
    out_specs = P("tm", "rows", None, None)
    return jax.shard_map(body, mesh=mesh, in_specs=in_specs, out_specs=out_specs, check_vma=False)
```

```python
import jax
import jax.numpy as jnp
from jax import lax
from jax.experimental import pallas as pl
from jax.experimental.pallas import tpu as pltpu
from jax.sharding import PartitionSpec as P

MESH = pl.DeviceIdType.MESH
BF = jnp.bfloat16
F32 = jnp.float32
F, R, W, C = 4, 4, 96, 192
LO, HI = 128, 64
K1 = 640


def norm_act(value, gain):
    lo, hi = value
    mean = jnp.sum(lo * lo + hi * hi, axis=-1, keepdims=True) * (1.0 / C)
    scale = lax.rsqrt(mean + 1e-06)
    return tuple(s / (1.0 + jnp.exp(-s)) for s in (lo * scale * gain[0], hi * scale * gain[1]))


def lane_id():
    return lax.broadcasted_iota(jnp.int32, (W, LO), 1)


def join(first, second):
    both = first[1] + pltpu.roll(second[1], HI, 1)
    return jnp.concatenate([first[0].astype(BF), second[0].astype(BF), both.astype(BF)], axis=1)


def split(packet):
    values = packet.astype(F32)
    tail = values[:, 2 * LO :]
    low = lane_id() < HI
    first = jnp.where(low, tail, 0.0)
    second = jnp.where(low, pltpu.roll(tail, HI, 1), 0.0)
    return (values[:, :LO], first), (values[:, LO : 2 * LO], second)


def widen(ref, value):
    column = lax.broadcasted_iota(jnp.int32, (W, LO), 0)
    lo, hi = value

    def left(v):
        return jnp.where(column == 0, 0.0, pltpu.roll(v, 1, 0))

    def right(v):
        return jnp.where(column == W - 1, 0.0, pltpu.roll(v, W - 1, 0))

    ref[:, 0:128] = left(lo).astype(BF)
    ref[:, 128:256] = lo.astype(BF)
    ref[:, 256:384] = right(lo).astype(BF)
    ref[:, 384:512] = (left(hi) + pltpu.roll(hi, HI, 1)).astype(BF)
    ref[:, 512:640] = right(hi).astype(BF)


def place():
    r, t = lax.axis_index("rows"), lax.axis_index("tm")
    r2, t2 = lax.div(r, 2), lax.div(t, 2)
    r1, t1 = lax.rem(r, 2), lax.rem(t, 2)
    return 2 * t2 + r1, 2 * r2 + t1, (2 * r2 + t1, 2 * t2 + r1), r1 != t1


def device(slab, strip):
    s2, q2 = lax.div(slab, 2), lax.div(strip, 2)
    return 2 * q2 + lax.rem(slab, 2), 2 * s2 + lax.rem(strip, 2)


def kernel(
    video, gains, kernels, out,
    vid, X, Wt, acc, own, swap_in, A, T, N, Q,
    w_sem, v_sem, l_sem, sw_send, sw_recv, t_send, t_recv, n_send, n_recv, q_send, q_recv,
):
    slab, strip, partner, swaps = place()
    has_prev, has_next = slab > 0, slab < 7
    has_up, has_down = strip > 0, strip < 31
    prev, follow = device(slab - 1, strip), device(slab + 1, strip)
    up, down = device(slab, strip - 1), device(slab, strip + 1)

    loads = [pltpu.make_async_copy(video.at[pl.ds(2, 2)], vid.at[pl.ds(2, 2)], v_sem.at[1]),
             pltpu.make_async_copy(video.at[pl.ds(0, 2)], vid.at[pl.ds(0, 2)], v_sem.at[0])]
    for copy in loads:
        copy.start()

    def weights(k):
        copies = [pltpu.make_async_copy(
            kernels.at[k, :, :, :, pl.ds(0, LO), :], Wt.at[k, :, :, pl.ds(0, 3), :, :], w_sem.at[k, 0])]
        for q in range(3):
            copies.append(pltpu.make_async_copy(
                kernels.at[k, :, :, q, pl.ds(LO, HI), :],
                Wt.at[k, :, :, 3 + q // 2, pl.ds(HI * (q % 2), HI), :],
                w_sem.at[k, 1 + q]))
        return copies

    zero = jnp.zeros((W, 2 * C), BF)
    for side, there in ((0, has_up), (1, has_down)):
        @pl.when(jnp.logical_not(there))
        def _(side=side):
            @pl.loop(0, 4)
            def _(j):
                N[j, 0, side] = zero
                N[j, 1, side] = zero
                Q[j, side] = zero

    @pl.when(jnp.logical_not(has_prev))
    def _():
        @pl.loop(0, 4)
        def _(j):
            for r in range(R):
                T[j, r] = zero
            for side in range(2):
                Q[j, side] = zero

    barrier = pltpu.get_barrier_semaphore()
    count = jnp.int32(0)
    for there, target in ((has_prev, prev), (has_next, follow), (has_up, up), (has_down, down), (swaps, partner)):
        count = count + there.astype(jnp.int32)

        @pl.when(there)
        def _(target=target):
            pl.semaphore_signal(barrier, inc=1, device_id=target, device_id_type=MESH)

    pl.semaphore_wait(barrier, count)

    def remote(src, dst, send, recv, target):
        return pltpu.make_async_remote_copy(
            src_ref=src, dst_ref=dst, send_sem=send, recv_sem=recv, device_id=target, device_id_type=MESH)

    def exchange(source, sink, n, p, r=None):
        at = (p,) if r is None else (p, r)
        sem = (n, p, 0) if r is None else (n, p, r)
        copy = remote(source.at[at], sink.at[at], sw_send.at[sem], sw_recv.at[sem], partner)
        local = pltpu.make_async_copy(source.at[at], sink.at[at], l_sem.at[sem])
        return copy, local

    def begin(pair):
        copy, local = pair

        @pl.when(swaps)
        def _():
            copy.start()

        @pl.when(jnp.logical_not(swaps))
        def _():
            local.start()

    def finish(pair):
        copy, local = pair

        @pl.when(swaps)
        def _():
            copy.wait_recv()

        @pl.when(jnp.logical_not(swaps))
        def _():
            local.wait()

    def packed(r, p):
        pair = []
        for f in range(2):
            whole = vid[2 * p + f, r].astype(F32)
            whole = jnp.concatenate([whole, jnp.zeros((W, HI), F32)], axis=1)
            pair.append((whole[:, :LO], whole[:, LO:]))
        own[p, r] = join(*pair)

    for q, load in enumerate(loads):
        p = 1 - q
        load.wait()

        @pl.loop(0, R)
        def _(r, p=p):
            packed(r, p)

        begin(exchange(own, swap_in, 0, p))

    for copy in weights(0):
        copy.start()

    @pl.loop(1, 4)
    def _(k):
        for copy in weights(k):
            copy.start()

    @pl.loop(0, 36)
    def _(i):
        Wt[lax.div(i, 9), lax.div(lax.rem(i, 9), 3), lax.rem(i, 3), 4, HI:, :] = jnp.zeros((LO - HI, C), BF)

    def gain(k):
        row = jnp.concatenate([gains[pl.ds(k, 1), :], jnp.zeros((1, HI), F32)], axis=1)
        return row[:, :LO], row[:, LO:]

    def frames_copy(j, r):
        return remote(A.at[j, 1, r], T.at[j, r], t_send.at[j, r], t_recv.at[j, r], follow)

    def row_copy(j, p, side):
        return remote(A.at[j, p, 3 * side], N.at[j, p, 1 - side], n_send.at[j, p, side], n_recv.at[j, p, 1 - side],
                      (up, down)[side])

    def corner_copy(j, side):
        return remote(T.at[j, 3 * side], Q.at[j, 1 - side], q_send.at[j, side], q_recv.at[j, 1 - side],
                      (up, down)[side])

    sides = ((0, has_up), (1, has_down))

    def send_rows(j, p):
        for side, there in sides:
            @pl.when(there)
            def _(side=side):
                row_copy(j, p, side).start()

    def send_frames(j):
        @pl.when(has_next)
        def _():
            for r in (0, 3, 1, 2):
                frames_copy(j, r).start()

    def emit(j, p, r, pair):
        for f in range(2):
            widen(X.at[lax.rem(j, 2), 2 + 2 * p + f, r + 1], pair[f])
        A[j, p, r] = join(*pair)

    def widen_packet(ref, j, f, r):
        pair = split(ref[...])
        for i in range(2):
            widen(X.at[lax.rem(j, 2), f + i, r], pair[i])

    def take_rows(j):
        for side, there in sides:
            @pl.when(there)
            def _(side=side):
                for p in (1, 0):
                    row_copy(j, p, 1 - side).wait_recv()

        for i in range(4):
            p, side = lax.div(i, 2), lax.rem(i, 2)
            widen_packet(N.at[j, p, side], j, 2 + 2 * p, 5 * side)

    def forward_corners(j):
        @pl.when(has_prev)
        def _():
            for side, there in sides:
                frames_copy(j, 3 * side).wait_recv()

                @pl.when(there)
                def _(side=side):
                    corner_copy(j, side).start()

    def take_frames(j):
        @pl.when(has_prev)
        def _():
            for r in (1, 2):
                frames_copy(j, r).wait_recv()

        @pl.loop(0, R)
        def _(r):
            widen_packet(T.at[j, r], j, 0, r + 1)

        for side, there in sides:
            @pl.when(jnp.logical_and(there, has_prev))
            def _(side=side):
                corner_copy(j, 1 - side).wait_recv()

        for side in range(2):
            widen_packet(Q.at[j, side], j, 0, 5 * side)

    def convolve(j, p, rows):
        s = lax.rem(j, 2)
        parts = []
        for dt in range(3):
            for dr in range(3):
                parts.append(jnp.concatenate(
                    [X[s, 2 * p + dt + f, r + dr] for f in range(2) for r in rows], axis=0))
        acc[...] = jnp.dot(
            jnp.concatenate(parts, axis=1), Wt[j].reshape(9 * K1, C), preferred_element_type=F32
        ).reshape(2, 2, W, C)

    def sums(f, i):
        return acc[f, i, :, 0:LO], jnp.concatenate([acc[f, i, :, LO:C], jnp.zeros((W, HI), F32)], axis=1)

    def after(j, p, rows):
        @pl.when(lax.rem(j, 2) == 1)
        def _():
            for i in range(2):
                r = rows[0] + i * (rows[1] - rows[0])
                old = split(swap_in[p, r])
                pair = [tuple((a + b).astype(BF).astype(F32) for a, b in zip(old[f], sums(f, i))) for f in range(2)]
                swap_in[p, r] = join(*pair)
                for f in range(2):
                    acc[f, i, :, 0:LO] = pair[f][0]
                    acc[f, i, :, LO:C] = pair[f][1][:, :HI]

        @pl.when(j < 3)
        def _():
            g = gain(j + 1)

            for i in range(2):
                r = rows[0] + i * (rows[1] - rows[0])
                emit(j + 1, p, r, [norm_act(sums(f, i), g) for f in range(2)])

    def outward(p, r):
        return exchange(swap_in, out, 1, p, r)

    g0 = gain(0)

    @pl.loop(0, 2)
    def _(q):
        p = 1 - q
        finish(exchange(own, swap_in, 0, p))

        for r in range(R):
            emit(0, p, r, [norm_act(v, g0) for v in split(swap_in[p, r])])

        send_rows(0, p)

        @pl.when(p == 1)
        def _():
            send_frames(0)

    def unit(u):
        first = jnp.where(jnp.logical_or(u == 1, u == 2), 0, 1)
        return 1 - lax.div(u, 2), (first, 3 - first)

    for j in range(4):
        for copy in weights(j):
            copy.wait()

        @pl.loop(0, 4)
        def _(u):
            p, rows = unit(u)

            @pl.when(u == 1)
            def _():
                take_rows(j)
                forward_corners(j)

            @pl.when(u == 2)
            def _():
                take_frames(j)

            convolve(j, p, rows)
            after(j, p, rows)

            @pl.when(jnp.logical_and(j < 3, jnp.logical_or(u == 1, u == 2)))
            def _():
                send_rows(j + 1, p)

            @pl.when(jnp.logical_and(j < 3, u == 1))
            def _():
                send_frames(j + 1)

            @pl.when(j == 3)
            def _():
                for r in rows:
                    begin(outward(p, r))

    @pl.loop(0, 2)
    def _(p):
        @pl.loop(0, R)
        def _(r):
            finish(outward(p, r))

    @pl.when(swaps)
    def _():
        @pl.loop(0, 2)
        def _(p):
            exchange(own, swap_in, 0, p)[0].wait_send()

            @pl.loop(0, R)
            def _(r):
                outward(p, r)[0].wait_send()

    @pl.loop(0, 4)
    def _(j):
        for side, there in sides:
            @pl.when(there)
            def _(side=side):
                for p in (1, 0):
                    row_copy(j, p, side).wait_send()

            @pl.when(jnp.logical_and(there, has_prev))
            def _(side=side):
                corner_copy(j, side).wait_send()

        @pl.when(has_next)
        def _():
            for r in range(R):
                frames_copy(j, r).wait_send()


def unpack(packets, out):
    for r in range(R):
        pair = split(packets[0, r])
        for f in range(2):
            out[f, r, :, 0:LO] = pair[f][0].astype(BF)
            out[f, r, :, LO:C] = pair[f][1][:, :HI].astype(BF)


def body(video, gains, kernels):
    packet = (W, 2 * C)
    dma = pltpu.SemaphoreType.DMA
    packets = pl.pallas_call(
        kernel,
        out_shape=jax.ShapeDtypeStruct((2, R) + packet, BF),
        in_specs=[
            pl.BlockSpec(memory_space=pl.ANY),
            pl.BlockSpec(memory_space=pltpu.VMEM),
            pl.BlockSpec(memory_space=pl.ANY),
        ],
        out_specs=pl.BlockSpec(memory_space=pl.ANY),
        scratch_shapes=[
            pltpu.VMEM((F, R, W, C), BF),
            pltpu.VMEM((2, F + 2, R + 2, W, K1), BF),
            pltpu.VMEM((4, 3, 3, 5, LO, C), BF),
            pltpu.VMEM((2, 2, W, C), F32),
            pltpu.VMEM((2, R) + packet, BF),
            pltpu.VMEM((2, R) + packet, BF),
            pltpu.VMEM((4, 2, R) + packet, BF),
            pltpu.VMEM((4, R) + packet, BF),
            pltpu.VMEM((4, 2, 2) + packet, BF),
            pltpu.VMEM((4, 2) + packet, BF),
            dma((4, 4)), dma((2,)), dma((2, 2, R)),
            dma((2, 2, R)), dma((2, 2, R)),
            dma((4, R)), dma((4, R)),
            dma((4, 2, 2)), dma((4, 2, 2)),
            dma((4, 2)), dma((4, 2)),
        ],
        compiler_params=pltpu.CompilerParams(
            collective_id=0, has_side_effects=True, vmem_limit_bytes=56 << 20),
        name="blocks",
    )(video, gains, kernels)
    return pl.pallas_call(
        unpack,
        out_shape=jax.ShapeDtypeStruct(video.shape, video.dtype),
        grid=(2,),
        in_specs=[pl.BlockSpec((1, R) + packet, lambda p: (p, 0, 0, 0))],
        out_specs=pl.BlockSpec((2, R, W, C), lambda p: (p, 0, 0, 0)),
        name="unpack",
    )(packets)


def solution(mesh):
    in_specs = (P("tm", "rows", None, None), P(), P())
    out_specs = P("tm", "rows", None, None)
    return jax.shard_map(body, mesh=mesh, in_specs=in_specs, out_specs=out_specs, check_vma=False)
```

```python
import jax
import jax.numpy as jnp
from jax import lax
from jax.experimental import pallas as pl
from jax.experimental.pallas import tpu as pltpu
from jax.sharding import PartitionSpec as P

MESH = pl.DeviceIdType.MESH
BF = jnp.bfloat16
F32 = jnp.float32
F, R, W, C = 4, 4, 96, 192
LO, HI = 128, 64
K1 = 640


def norm_act(value, gain):
    lo, hi = value
    mean = jnp.sum(lo * lo + hi * hi, axis=-1, keepdims=True) * (1.0 / C)
    scale = lax.rsqrt(mean + 1e-06)
    return tuple(s / (1.0 + jnp.exp(-s)) for s in (lo * scale * gain[0], hi * scale * gain[1]))


def lane_id():
    return lax.broadcasted_iota(jnp.int32, (W, LO), 1)


def join(first, second):
    both = first[1] + pltpu.roll(second[1], HI, 1)
    return jnp.concatenate([first[0].astype(BF), second[0].astype(BF), both.astype(BF)], axis=1)


def split(packet):
    values = packet.astype(F32)
    tail = values[:, 2 * LO :]
    low = lane_id() < HI
    first = jnp.where(low, tail, 0.0)
    second = jnp.where(low, pltpu.roll(tail, HI, 1), 0.0)
    return (values[:, :LO], first), (values[:, LO : 2 * LO], second)


def widen(ref, value):
    column = lax.broadcasted_iota(jnp.int32, (W, LO), 0)
    lo, hi = value

    def left(v):
        return jnp.where(column == 0, 0.0, pltpu.roll(v, 1, 0))

    def right(v):
        return jnp.where(column == W - 1, 0.0, pltpu.roll(v, W - 1, 0))

    ref[:, 0:128] = left(lo).astype(BF)
    ref[:, 128:256] = lo.astype(BF)
    ref[:, 256:384] = right(lo).astype(BF)
    ref[:, 384:512] = (left(hi) + pltpu.roll(hi, HI, 1)).astype(BF)
    ref[:, 512:640] = right(hi).astype(BF)


def place():
    r, t = lax.axis_index("rows"), lax.axis_index("tm")
    r2, t2 = lax.div(r, 2), lax.div(t, 2)
    r1, t1 = lax.rem(r, 2), lax.rem(t, 2)
    return 2 * t2 + r1, 2 * r2 + t1, (2 * r2 + t1, 2 * t2 + r1), r1 != t1


def device(slab, strip):
    s2, q2 = lax.div(slab, 2), lax.div(strip, 2)
    return 2 * q2 + lax.rem(slab, 2), 2 * s2 + lax.rem(strip, 2)


def kernel(
    video, gains, kernels, out,
    vid, X, Wt, acc, own, swap_in, A, T, N, Q,
    w_sem, v_sem, l_sem, sw_send, sw_recv, t_send, t_recv, n_send, n_recv, q_send, q_recv,
):
    slab, strip, partner, swaps = place()
    has_prev, has_next = slab > 0, slab < 7
    has_up, has_down = strip > 0, strip < 31
    prev, follow = device(slab - 1, strip), device(slab + 1, strip)
    up, down = device(slab, strip - 1), device(slab, strip + 1)

    loads = [pltpu.make_async_copy(video.at[pl.ds(2, 2)], vid.at[pl.ds(2, 2)], v_sem.at[1]),
             pltpu.make_async_copy(video.at[pl.ds(0, 2)], vid.at[pl.ds(0, 2)], v_sem.at[0])]
    for copy in loads:
        copy.start()

    def weights(k):
        copies = [pltpu.make_async_copy(
            kernels.at[k, :, :, :, pl.ds(0, LO), :], Wt.at[k, :, :, pl.ds(0, 3), :, :], w_sem.at[k, 0])]
        for q in range(3):
            copies.append(pltpu.make_async_copy(
                kernels.at[k, :, :, q, pl.ds(LO, HI), :],
                Wt.at[k, :, :, 3 + q // 2, pl.ds(HI * (q % 2), HI), :],
                w_sem.at[k, 1 + q]))
        return copies

    zero = jnp.zeros((W, 2 * C), BF)
    for side, there in ((0, has_up), (1, has_down)):
        @pl.when(jnp.logical_not(there))
        def _(side=side):
            @pl.loop(0, 4)
            def _(j):
                N[j, 0, side] = zero
                N[j, 1, side] = zero
                Q[j, side] = zero

    @pl.when(jnp.logical_not(has_prev))
    def _():
        @pl.loop(0, 4)
        def _(j):
            for r in range(R):
                T[j, r] = zero
            for side in range(2):
                Q[j, side] = zero

    barrier = pltpu.get_barrier_semaphore()
    count = jnp.int32(0)
    for there, target in ((has_prev, prev), (has_next, follow), (has_up, up), (has_down, down), (swaps, partner)):
        count = count + there.astype(jnp.int32)

        @pl.when(there)
        def _(target=target):
            pl.semaphore_signal(barrier, inc=1, device_id=target, device_id_type=MESH)

    pl.semaphore_wait(barrier, count)

    def remote(src, dst, send, recv, target):
        return pltpu.make_async_remote_copy(
            src_ref=src, dst_ref=dst, send_sem=send, recv_sem=recv, device_id=target, device_id_type=MESH)

    def exchange(source, sink, n, p, r=None):
        at = (p,) if r is None else (p, r)
        sem = (n, p, 0) if r is None else (n, p, r)
        copy = remote(source.at[at], sink.at[at], sw_send.at[sem], sw_recv.at[sem], partner)
        local = pltpu.make_async_copy(source.at[at], sink.at[at], l_sem.at[sem])
        return copy, local

    def begin(pair):
        copy, local = pair

        @pl.when(swaps)
        def _():
            copy.start()

        @pl.when(jnp.logical_not(swaps))
        def _():
            local.start()

    def finish(pair):
        copy, local = pair

        @pl.when(swaps)
        def _():
            copy.wait_recv()

        @pl.when(jnp.logical_not(swaps))
        def _():
            local.wait()

    def packed(r, p):
        pair = []
        for f in range(2):
            whole = vid[2 * p + f, r].astype(F32)
            whole = jnp.concatenate([whole, jnp.zeros((W, HI), F32)], axis=1)
            pair.append((whole[:, :LO], whole[:, LO:]))
        own[p, r] = join(*pair)

    for q, load in enumerate(loads):
        p = 1 - q
        load.wait()

        @pl.loop(0, R)
        def _(r, p=p):
            packed(r, p)

        begin(exchange(own, swap_in, 0, p))

    for copy in weights(0):
        copy.start()

    @pl.loop(1, 4)
    def _(k):
        for copy in weights(k):
            copy.start()

    @pl.loop(0, 36)
    def _(i):
        Wt[lax.div(i, 9), lax.div(lax.rem(i, 9), 3), lax.rem(i, 3), 4, HI:, :] = jnp.zeros((LO - HI, C), BF)

    def gain(k):
        row = jnp.concatenate([gains[pl.ds(k, 1), :], jnp.zeros((1, HI), F32)], axis=1)
        return row[:, :LO], row[:, LO:]

    def frames_copy(j, r):
        return remote(A.at[j, 1, r], T.at[j, r], t_send.at[j, r], t_recv.at[j, r], follow)

    def row_copy(j, p, side):
        return remote(A.at[j, p, 3 * side], N.at[j, p, 1 - side], n_send.at[j, p, side], n_recv.at[j, p, 1 - side],
                      (up, down)[side])

    def corner_copy(j, side):
        return remote(T.at[j, 3 * side], Q.at[j, 1 - side], q_send.at[j, side], q_recv.at[j, 1 - side],
                      (up, down)[side])

    sides = ((0, has_up), (1, has_down))

    def send_rows(j, p):
        for side, there in sides:
            @pl.when(there)
            def _(side=side):
                row_copy(j, p, side).start()

    def send_frames(j):
        @pl.when(has_next)
        def _():
            for r in (0, 3, 1, 2):
                frames_copy(j, r).start()

    def emit(j, p, r, pair):
        for f in range(2):
            widen(X.at[lax.rem(j, 2), 2 + 2 * p + f, r + 1], pair[f])
        A[j, p, r] = join(*pair)

    def widen_packet(ref, j, f, r):
        pair = split(ref[...])
        for i in range(2):
            widen(X.at[lax.rem(j, 2), f + i, r], pair[i])

    def take_rows(j):
        for side, there in sides:
            @pl.when(there)
            def _(side=side):
                for p in (1, 0):
                    row_copy(j, p, 1 - side).wait_recv()

        for i in range(4):
            p, side = lax.div(i, 2), lax.rem(i, 2)
            widen_packet(N.at[j, p, side], j, 2 + 2 * p, 5 * side)

    def forward_corners(j):
        @pl.when(has_prev)
        def _():
            for side, there in sides:
                frames_copy(j, 3 * side).wait_recv()

                @pl.when(there)
                def _(side=side):
                    corner_copy(j, side).start()

    def take_frames(j):
        @pl.when(has_prev)
        def _():
            for r in (1, 2):
                frames_copy(j, r).wait_recv()

        @pl.loop(0, R)
        def _(r):
            widen_packet(T.at[j, r], j, 0, r + 1)

        for side, there in sides:
            @pl.when(jnp.logical_and(there, has_prev))
            def _(side=side):
                corner_copy(j, 1 - side).wait_recv()

        for side in range(2):
            widen_packet(Q.at[j, side], j, 0, 5 * side)

    def convolve(j, p, rows):
        s = lax.rem(j, 2)
        parts = []
        for dt in range(3):
            for dr in range(3):
                parts.append(jnp.concatenate(
                    [X[s, 2 * p + dt + f, r + dr] for f in range(2) for r in rows], axis=0))
        acc[...] = jnp.dot(
            jnp.concatenate(parts, axis=1), Wt[j].reshape(9 * K1, C), preferred_element_type=F32
        ).reshape(2, 2, W, C)

    def sums(f, i):
        return acc[f, i, :, 0:LO], jnp.concatenate([acc[f, i, :, LO:C], jnp.zeros((W, HI), F32)], axis=1)

    def after(j, p, rows):
        @pl.when(lax.rem(j, 2) == 1)
        def _():
            for i in range(2):
                r = rows[0] + i * (rows[1] - rows[0])
                old = split(swap_in[p, r])
                pair = [tuple((a + b).astype(BF).astype(F32) for a, b in zip(old[f], sums(f, i))) for f in range(2)]
                swap_in[p, r] = join(*pair)
                for f in range(2):
                    acc[f, i, :, 0:LO] = pair[f][0]
                    acc[f, i, :, LO:C] = pair[f][1][:, :HI]

        @pl.when(j < 3)
        def _():
            g = gain(j + 1)

            for i in range(2):
                r = rows[0] + i * (rows[1] - rows[0])
                emit(j + 1, p, r, [norm_act(sums(f, i), g) for f in range(2)])

    def outward(p, r):
        return exchange(swap_in, out, 1, p, r)

    g0 = gain(0)

    @pl.loop(0, 2)
    def _(q):
        p = 1 - q
        finish(exchange(own, swap_in, 0, p))

        for r in range(R):
            emit(0, p, r, [norm_act(v, g0) for v in split(swap_in[p, r])])

        send_rows(0, p)

        @pl.when(p == 1)
        def _():
            send_frames(0)

    def unit(u):
        first = jnp.where(jnp.logical_or(u == 1, u == 2), 0, 1)
        return 1 - lax.div(u, 2), (first, 3 - first)

    for j in range(4):
        for copy in weights(j):
            copy.wait()

        @pl.loop(0, 4)
        def _(u):
            p, rows = unit(u)

            @pl.when(u == jnp.where(j == 0, 1, 0))
            def _():
                forward_corners(j)

            @pl.when(u == 1)
            def _():
                take_rows(j)

            @pl.when(u == 2)
            def _():
                take_frames(j)

            convolve(j, p, rows)
            after(j, p, rows)

            @pl.when(jnp.logical_and(j < 3, jnp.logical_or(u == 1, u == 2)))
            def _():
                send_rows(j + 1, p)

            @pl.when(jnp.logical_and(j < 3, u == 1))
            def _():
                send_frames(j + 1)

            @pl.when(j == 3)
            def _():
                for r in rows:
                    begin(outward(p, r))

    @pl.loop(0, 2)
    def _(p):
        @pl.loop(0, R)
        def _(r):
            finish(outward(p, r))

    @pl.when(swaps)
    def _():
        @pl.loop(0, 2)
        def _(p):
            exchange(own, swap_in, 0, p)[0].wait_send()

            @pl.loop(0, R)
            def _(r):
                outward(p, r)[0].wait_send()

    @pl.loop(0, 4)
    def _(j):
        for side, there in sides:
            @pl.when(there)
            def _(side=side):
                for p in (1, 0):
                    row_copy(j, p, side).wait_send()

            @pl.when(jnp.logical_and(there, has_prev))
            def _(side=side):
                corner_copy(j, side).wait_send()

        @pl.when(has_next)
        def _():
            for r in range(R):
                frames_copy(j, r).wait_send()


def unpack(packets, out):
    for r in range(R):
        pair = split(packets[0, r])
        for f in range(2):
            out[f, r, :, 0:LO] = pair[f][0].astype(BF)
            out[f, r, :, LO:C] = pair[f][1][:, :HI].astype(BF)


def body(video, gains, kernels):
    packet = (W, 2 * C)
    dma = pltpu.SemaphoreType.DMA
    packets = pl.pallas_call(
        kernel,
        out_shape=jax.ShapeDtypeStruct((2, R) + packet, BF),
        in_specs=[
            pl.BlockSpec(memory_space=pl.ANY),
            pl.BlockSpec(memory_space=pltpu.VMEM),
            pl.BlockSpec(memory_space=pl.ANY),
        ],
        out_specs=pl.BlockSpec(memory_space=pl.ANY),
        scratch_shapes=[
            pltpu.VMEM((F, R, W, C), BF),
            pltpu.VMEM((2, F + 2, R + 2, W, K1), BF),
            pltpu.VMEM((4, 3, 3, 5, LO, C), BF),
            pltpu.VMEM((2, 2, W, C), F32),
            pltpu.VMEM((2, R) + packet, BF),
            pltpu.VMEM((2, R) + packet, BF),
            pltpu.VMEM((4, 2, R) + packet, BF),
            pltpu.VMEM((4, R) + packet, BF),
            pltpu.VMEM((4, 2, 2) + packet, BF),
            pltpu.VMEM((4, 2) + packet, BF),
            dma((4, 4)), dma((2,)), dma((2, 2, R)),
            dma((2, 2, R)), dma((2, 2, R)),
            dma((4, R)), dma((4, R)),
            dma((4, 2, 2)), dma((4, 2, 2)),
            dma((4, 2)), dma((4, 2)),
        ],
        compiler_params=pltpu.CompilerParams(
            collective_id=0, has_side_effects=True, vmem_limit_bytes=56 << 20),
        name="blocks",
    )(video, gains, kernels)
    return pl.pallas_call(
        unpack,
        out_shape=jax.ShapeDtypeStruct(video.shape, video.dtype),
        grid=(2,),
        in_specs=[pl.BlockSpec((1, R) + packet, lambda p: (p, 0, 0, 0))],
        out_specs=pl.BlockSpec((2, R, W, C), lambda p: (p, 0, 0, 0)),
        name="unpack",
    )(packets)


def solution(mesh):
    in_specs = (P("tm", "rows", None, None), P(), P())
    out_specs = P("tm", "rows", None, None)
    return jax.shard_map(body, mesh=mesh, in_specs=in_specs, out_specs=out_specs, check_vma=False)
```

```python
import jax
import jax.numpy as jnp
from jax import lax
from jax.experimental import pallas as pl
from jax.experimental.pallas import tpu as pltpu
from jax.sharding import PartitionSpec as P

MESH = pl.DeviceIdType.MESH
BF = jnp.bfloat16
F32 = jnp.float32
F, R, W, C = 4, 4, 96, 192
LO, HI = 128, 64
K1 = 640


def norm_act(value, gain):
    lo, hi = value
    mean = jnp.sum(lo * lo + hi * hi, axis=-1, keepdims=True) * (1.0 / C)
    scale = lax.rsqrt(mean + 1e-06)
    return tuple(s / (1.0 + jnp.exp(-s)) for s in (lo * scale * gain[0], hi * scale * gain[1]))


def lane_id():
    return lax.broadcasted_iota(jnp.int32, (W, LO), 1)


def join(first, second):
    both = first[1] + pltpu.roll(second[1], HI, 1)
    return jnp.concatenate([first[0].astype(BF), second[0].astype(BF), both.astype(BF)], axis=1)


def split(packet):
    values = packet.astype(F32)
    tail = values[:, 2 * LO :]
    low = lane_id() < HI
    first = jnp.where(low, tail, 0.0)
    second = jnp.where(low, pltpu.roll(tail, HI, 1), 0.0)
    return (values[:, :LO], first), (values[:, LO : 2 * LO], second)


def widen(ref, value):
    column = lax.broadcasted_iota(jnp.int32, (W, LO), 0)
    lo, hi = value

    def left(v):
        return jnp.where(column == 0, 0.0, pltpu.roll(v, 1, 0))

    def right(v):
        return jnp.where(column == W - 1, 0.0, pltpu.roll(v, W - 1, 0))

    ref[:, 0:128] = left(lo).astype(BF)
    ref[:, 128:256] = lo.astype(BF)
    ref[:, 256:384] = right(lo).astype(BF)
    ref[:, 384:512] = (left(hi) + pltpu.roll(hi, HI, 1)).astype(BF)
    ref[:, 512:640] = right(hi).astype(BF)


def place():
    r, t = lax.axis_index("rows"), lax.axis_index("tm")
    r2, t2 = lax.div(r, 2), lax.div(t, 2)
    r1, t1 = lax.rem(r, 2), lax.rem(t, 2)
    return 2 * t2 + r1, 2 * r2 + t1, (2 * r2 + t1, 2 * t2 + r1), r1 != t1


def device(slab, strip):
    s2, q2 = lax.div(slab, 2), lax.div(strip, 2)
    return 2 * q2 + lax.rem(slab, 2), 2 * s2 + lax.rem(strip, 2)


def kernel(
    video, gains, kernels, out,
    vid, X, Wt, acc, own, swap_in, A, T, N, Q,
    w_sem, v_sem, l_sem, sw_send, sw_recv, t_send, t_recv, n_send, n_recv, q_send, q_recv,
):
    slab, strip, partner, swaps = place()
    has_prev, has_next = slab > 0, slab < 7
    has_up, has_down = strip > 0, strip < 31
    prev, follow = device(slab - 1, strip), device(slab + 1, strip)
    up, down = device(slab, strip - 1), device(slab, strip + 1)

    loads = [pltpu.make_async_copy(video.at[pl.ds(2, 2)], vid.at[pl.ds(2, 2)], v_sem.at[1]),
             pltpu.make_async_copy(video.at[pl.ds(0, 2)], vid.at[pl.ds(0, 2)], v_sem.at[0])]
    for copy in loads:
        copy.start()

    def weights(k):
        copies = [pltpu.make_async_copy(
            kernels.at[k, :, :, :, pl.ds(0, LO), :], Wt.at[k, :, :, pl.ds(0, 3), :, :], w_sem.at[k, 0])]
        for q in range(3):
            copies.append(pltpu.make_async_copy(
                kernels.at[k, :, :, q, pl.ds(LO, HI), :],
                Wt.at[k, :, :, 3 + q // 2, pl.ds(HI * (q % 2), HI), :],
                w_sem.at[k, 1 + q]))
        return copies

    zero = jnp.zeros((W, 2 * C), BF)
    for side, there in ((0, has_up), (1, has_down)):
        @pl.when(jnp.logical_not(there))
        def _(side=side):
            @pl.loop(0, 4)
            def _(j):
                N[j, 0, side] = zero
                N[j, 1, side] = zero
                Q[j, side] = zero

    @pl.when(jnp.logical_not(has_prev))
    def _():
        @pl.loop(0, 4)
        def _(j):
            for r in range(R):
                T[j, r] = zero
            for side in range(2):
                Q[j, side] = zero

    barrier = pltpu.get_barrier_semaphore()
    count = jnp.int32(0)
    for there, target in ((has_prev, prev), (has_next, follow), (has_up, up), (has_down, down), (swaps, partner)):
        count = count + there.astype(jnp.int32)

        @pl.when(there)
        def _(target=target):
            pl.semaphore_signal(barrier, inc=1, device_id=target, device_id_type=MESH)

    pl.semaphore_wait(barrier, count)

    def remote(src, dst, send, recv, target):
        return pltpu.make_async_remote_copy(
            src_ref=src, dst_ref=dst, send_sem=send, recv_sem=recv, device_id=target, device_id_type=MESH)

    def exchange(source, sink, n, p, r=None):
        at = (p,) if r is None else (p, r)
        sem = (n, p, 0) if r is None else (n, p, r)
        copy = remote(source.at[at], sink.at[at], sw_send.at[sem], sw_recv.at[sem], partner)
        local = pltpu.make_async_copy(source.at[at], sink.at[at], l_sem.at[sem])
        return copy, local

    def begin(pair):
        copy, local = pair

        @pl.when(swaps)
        def _():
            copy.start()

        @pl.when(jnp.logical_not(swaps))
        def _():
            local.start()

    def finish(pair):
        copy, local = pair

        @pl.when(swaps)
        def _():
            copy.wait_recv()

        @pl.when(jnp.logical_not(swaps))
        def _():
            local.wait()

    def packed(r, p):
        pair = []
        for f in range(2):
            whole = vid[2 * p + f, r].astype(F32)
            whole = jnp.concatenate([whole, jnp.zeros((W, HI), F32)], axis=1)
            pair.append((whole[:, :LO], whole[:, LO:]))
        own[p, r] = join(*pair)

    for q, load in enumerate(loads):
        p = 1 - q
        load.wait()

        @pl.loop(0, R)
        def _(r, p=p):
            packed(r, p)
            begin(exchange(own, swap_in, 0, p, r))

    for copy in weights(0):
        copy.start()

    @pl.loop(1, 4)
    def _(k):
        for copy in weights(k):
            copy.start()

    @pl.loop(0, 36)
    def _(i):
        Wt[lax.div(i, 9), lax.div(lax.rem(i, 9), 3), lax.rem(i, 3), 4, HI:, :] = jnp.zeros((LO - HI, C), BF)

    def gain(k):
        row = jnp.concatenate([gains[pl.ds(k, 1), :], jnp.zeros((1, HI), F32)], axis=1)
        return row[:, :LO], row[:, LO:]

    def frames_copy(j, r):
        return remote(A.at[j, 1, r], T.at[j, r], t_send.at[j, r], t_recv.at[j, r], follow)

    def row_copy(j, p, side):
        return remote(A.at[j, p, 3 * side], N.at[j, p, 1 - side], n_send.at[j, p, side], n_recv.at[j, p, 1 - side],
                      (up, down)[side])

    def corner_copy(j, side):
        return remote(T.at[j, 3 * side], Q.at[j, 1 - side], q_send.at[j, side], q_recv.at[j, 1 - side],
                      (up, down)[side])

    sides = ((0, has_up), (1, has_down))

    def send_rows(j, p):
        for side, there in sides:
            @pl.when(there)
            def _(side=side):
                row_copy(j, p, side).start()

    def send_frames(j):
        @pl.when(has_next)
        def _():
            for r in (0, 3, 1, 2):
                frames_copy(j, r).start()

    def emit(j, p, r, pair):
        for f in range(2):
            widen(X.at[lax.rem(j, 2), 2 + 2 * p + f, r + 1], pair[f])
        A[j, p, r] = join(*pair)

    def widen_packet(ref, j, f, r):
        pair = split(ref[...])
        for i in range(2):
            widen(X.at[lax.rem(j, 2), f + i, r], pair[i])

    def take_rows(j):
        for side, there in sides:
            @pl.when(there)
            def _(side=side):
                for p in (1, 0):
                    row_copy(j, p, 1 - side).wait_recv()

        for i in range(4):
            p, side = lax.div(i, 2), lax.rem(i, 2)
            widen_packet(N.at[j, p, side], j, 2 + 2 * p, 5 * side)

    def forward_corners(j):
        @pl.when(has_prev)
        def _():
            for side, there in sides:
                frames_copy(j, 3 * side).wait_recv()

                @pl.when(there)
                def _(side=side):
                    corner_copy(j, side).start()

    def take_frames(j):
        @pl.when(has_prev)
        def _():
            for r in (1, 2):
                frames_copy(j, r).wait_recv()

        @pl.loop(0, R)
        def _(r):
            widen_packet(T.at[j, r], j, 0, r + 1)

        for side, there in sides:
            @pl.when(jnp.logical_and(there, has_prev))
            def _(side=side):
                corner_copy(j, 1 - side).wait_recv()

        for side in range(2):
            widen_packet(Q.at[j, side], j, 0, 5 * side)

    def convolve(j, p, rows):
        s = lax.rem(j, 2)
        parts = []
        for dt in range(3):
            for dr in range(3):
                parts.append(jnp.concatenate(
                    [X[s, 2 * p + dt + f, r + dr] for f in range(2) for r in rows], axis=0))
        acc[...] = jnp.dot(
            jnp.concatenate(parts, axis=1), Wt[j].reshape(9 * K1, C), preferred_element_type=F32
        ).reshape(2, 2, W, C)

    def sums(f, i):
        return acc[f, i, :, 0:LO], jnp.concatenate([acc[f, i, :, LO:C], jnp.zeros((W, HI), F32)], axis=1)

    def after(j, p, rows):
        @pl.when(lax.rem(j, 2) == 1)
        def _():
            for i in range(2):
                r = rows[0] + i * (rows[1] - rows[0])
                old = split(swap_in[p, r])
                pair = [tuple((a + b).astype(BF).astype(F32) for a, b in zip(old[f], sums(f, i))) for f in range(2)]
                swap_in[p, r] = join(*pair)
                for f in range(2):
                    acc[f, i, :, 0:LO] = pair[f][0]
                    acc[f, i, :, LO:C] = pair[f][1][:, :HI]

        @pl.when(j < 3)
        def _():
            g = gain(j + 1)

            for i in range(2):
                r = rows[0] + i * (rows[1] - rows[0])
                emit(j + 1, p, r, [norm_act(sums(f, i), g) for f in range(2)])

    def outward(p, r):
        return exchange(swap_in, out, 1, p, r)

    g0 = gain(0)

    @pl.loop(0, 2)
    def _(q):
        p = 1 - q
        for r in range(R):
            finish(exchange(own, swap_in, 0, p, r))
            emit(0, p, r, [norm_act(v, g0) for v in split(swap_in[p, r])])

        send_rows(0, p)

        @pl.when(p == 1)
        def _():
            send_frames(0)

    def unit(u):
        first = jnp.where(jnp.logical_or(u == 1, u == 2), 0, 1)
        return 1 - lax.div(u, 2), (first, 3 - first)

    for j in range(4):
        for copy in weights(j):
            copy.wait()

        @pl.loop(0, 4)
        def _(u):
            p, rows = unit(u)

            @pl.when(u == jnp.where(j == 0, 1, 0))
            def _():
                forward_corners(j)

            @pl.when(u == 1)
            def _():
                take_rows(j)

            @pl.when(u == 2)
            def _():
                take_frames(j)

            convolve(j, p, rows)
            after(j, p, rows)

            @pl.when(jnp.logical_and(j < 3, jnp.logical_or(u == 1, u == 2)))
            def _():
                send_rows(j + 1, p)

            @pl.when(jnp.logical_and(j < 3, u == 1))
            def _():
                send_frames(j + 1)

            @pl.when(j == 3)
            def _():
                for r in rows:
                    begin(outward(p, r))

    @pl.loop(0, 2)
    def _(p):
        @pl.loop(0, R)
        def _(r):
            finish(outward(p, r))

    @pl.when(swaps)
    def _():
        @pl.loop(0, 2)
        def _(p):
            @pl.loop(0, R)
            def _(r):
                exchange(own, swap_in, 0, p, r)[0].wait_send()
                outward(p, r)[0].wait_send()

    @pl.loop(0, 4)
    def _(j):
        for side, there in sides:
            @pl.when(there)
            def _(side=side):
                for p in (1, 0):
                    row_copy(j, p, side).wait_send()

            @pl.when(jnp.logical_and(there, has_prev))
            def _(side=side):
                corner_copy(j, side).wait_send()

        @pl.when(has_next)
        def _():
            for r in range(R):
                frames_copy(j, r).wait_send()


def unpack(packets, out):
    for r in range(R):
        pair = split(packets[0, r])
        for f in range(2):
            out[f, r, :, 0:LO] = pair[f][0].astype(BF)
            out[f, r, :, LO:C] = pair[f][1][:, :HI].astype(BF)


def body(video, gains, kernels):
    packet = (W, 2 * C)
    dma = pltpu.SemaphoreType.DMA
    packets = pl.pallas_call(
        kernel,
        out_shape=jax.ShapeDtypeStruct((2, R) + packet, BF),
        in_specs=[
            pl.BlockSpec(memory_space=pl.ANY),
            pl.BlockSpec(memory_space=pltpu.VMEM),
            pl.BlockSpec(memory_space=pl.ANY),
        ],
        out_specs=pl.BlockSpec(memory_space=pl.ANY),
        scratch_shapes=[
            pltpu.VMEM((F, R, W, C), BF),
            pltpu.VMEM((2, F + 2, R + 2, W, K1), BF),
            pltpu.VMEM((4, 3, 3, 5, LO, C), BF),
            pltpu.VMEM((2, 2, W, C), F32),
            pltpu.VMEM((2, R) + packet, BF),
            pltpu.VMEM((2, R) + packet, BF),
            pltpu.VMEM((4, 2, R) + packet, BF),
            pltpu.VMEM((4, R) + packet, BF),
            pltpu.VMEM((4, 2, 2) + packet, BF),
            pltpu.VMEM((4, 2) + packet, BF),
            dma((4, 4)), dma((2,)), dma((2, 2, R)),
            dma((2, 2, R)), dma((2, 2, R)),
            dma((4, R)), dma((4, R)),
            dma((4, 2, 2)), dma((4, 2, 2)),
            dma((4, 2)), dma((4, 2)),
        ],
        compiler_params=pltpu.CompilerParams(
            collective_id=0, has_side_effects=True, vmem_limit_bytes=56 << 20),
        name="blocks",
    )(video, gains, kernels)
    return pl.pallas_call(
        unpack,
        out_shape=jax.ShapeDtypeStruct(video.shape, video.dtype),
        grid=(2,),
        in_specs=[pl.BlockSpec((1, R) + packet, lambda p: (p, 0, 0, 0))],
        out_specs=pl.BlockSpec((2, R, W, C), lambda p: (p, 0, 0, 0)),
        name="unpack",
    )(packets)


def solution(mesh):
    in_specs = (P("tm", "rows", None, None), P(), P())
    out_specs = P("tm", "rows", None, None)
    return jax.shard_map(body, mesh=mesh, in_specs=in_specs, out_specs=out_specs, check_vma=False)
```
